128 devices in a mesh: expert: 16 (over z, y), group: 8 (over x, core).
Axes of the slice: x: 4, y: 4, z: 4, core: 2. Of those that a mesh axis runs over, the one named last changes fastest.
Arguments:
- tokens: bfloat16 [2, 16384, 2048], P(None, ('expert', 'group')), may hold values from -6 to 6
- expert_ids: int32 [2, 16384, 8], P(None, ('expert', 'group')), may hold values from 0 to 127, all different within a row; in each aligned block of 128 rows (0 to 127, 128 to 255, ..., all dimensions but the last counted through in order) at most 10 rows name the same one
- gate_probs: float32 [2, 16384, 8], P(None, ('expert', 'group')), may hold values from 0.05 to 1
- capacity: int32 [128], P(('expert', 'group')), may hold values from 448 to 896, as said below
- flows: int32 [128, 3], P(('expert', 'group')), may hold values from 0 to 64, as said below
- w_gate: bfloat16 [128, 2048, 768], P(('expert', 'group')), may hold values from -0.125 to 0.125
- w_up: bfloat16 [128, 2048, 768], P(('expert', 'group')), may hold values from -0.125 to 0.125
- w_down: bfloat16 [128, 768, 2048], P(('expert', 'group')), may hold values from -0.21875 to 0.21875
Outputs:
- mixed: bfloat16 [2, 16384, 2048], P(None, ('expert', 'group'))
The draws below stay inside these ranges and needn't reach their ends.
Inputs may be any that keep to these rules, and one draw needn't show every extreme that they name: `expert_ids`: among one device's 128 tokens of a micro-batch no expert is chosen more than 10 times, a bound that some block reaches; a token never chooses an expert twice. Some expert has capacity exactly 896. `flows`: some expert has all its grants exactly 64, the same expert that has capacity 896.
All inputs are finite; a program needn't handle non-finite values.
Results may differ from the reference program's by a relative error of at most 0.0085.
Values may be sent and summed in bfloat16 or wider, within the bound.
No kernel may reach another device: no remote copies, remote signals or barrier semaphores. Data moves between devices by JAX's collectives and lax.ppermute only.
A program may use at most 128 MiB of HBM per device.

```python
import math
import jax
import jax.numpy as jnp
import numpy as np
from jax import lax

D = 2048
FF = 768
TOPK = 8
TOK_DEV = 128
MICRO = 2
PARTNERS = 3
EXPERTS = 128
TOKENS = 16384
SLOTS = 10
CAP_MAX = 896
FLOW_MAX = 64


def chosen_expert(key):
    return jax.random.randint(jax.random.fold_in(key, 11), (), 0, EXPERTS)


def draw_capacity(key, part):
    drawn = jax.random.randint(jax.random.fold_in(key, 3), (EXPERTS,), CAP_MAX // 2, CAP_MAX + 1)
    return jnp.where(jnp.arange(EXPERTS) == chosen_expert(key), CAP_MAX, drawn).astype(jnp.int32)


def draw_flows(key, part):
    drawn = jax.random.randint(jax.random.fold_in(key, 5), (EXPERTS, PARTNERS), 0, FLOW_MAX + 1)
    picked = (jnp.arange(EXPERTS) == chosen_expert(key))[:, None]
    return jnp.where(picked, FLOW_MAX, drawn).astype(jnp.int32)


def level_of(stream_key, shape, cuts, low, top_value):
    level = 1.0
    for axis_at, parts in cuts:
        draws = jax.random.uniform(jax.random.fold_in(jax.random.fold_in(stream_key, 6), axis_at), (parts,), jnp.float32, low / len(cuts), top_value / len(cuts))
        level = level * jnp.repeat(jnp.exp(draws), shape[axis_at] // parts).reshape((-1,) + (1,) * (len(shape) - 1 - axis_at))
    return level


def deal_out(rng, own, number, rows, number_of, top, reach, slope):
    ranking = jax.random.permutation(rng, number_of)
    crowded, ordinary = shares(number_of, rows * top, reach, slope, True), shares(number_of, rows * top, reach, slope, False)
    places = jnp.arange(number_of)

    def named(tallies, rotation):
        used = int((tallies > 0).sum())
        fixed = max(1, used // 4)
        moved = fixed + (places - fixed + rotation * (used - fixed)) % max(1, number_of - fixed)
        return jnp.zeros((number_of,), jnp.int32).at[ranking[jnp.where(places < fixed, places, moved)]].set(jnp.asarray(tallies, jnp.int32))

    tallies = jnp.where(number % 4 == 0, named(crowded, number // 4), named(ordinary, number - number // 4 - 1))
    mixed = jax.random.permutation(jax.random.fold_in(own, 3), number_of)
    giver, receiver = mixed[0:number_of // 2 * 2:2], mixed[1:number_of // 2 * 2:2]
    slack = jnp.minimum(tallies[giver] - 1, reach - tallies[receiver]) // 2
    slack = jnp.where((giver == ranking[0]) | (receiver == ranking[0]) | (tallies[receiver] == 0), 0, jnp.maximum(slack, 0))
    moved = jax.random.randint(jax.random.fold_in(own, 4), (number_of // 2,), 0, 1 << 20) % (slack + 1)
    tallies = tallies.at[giver].add(-moved).at[receiver].add(moved)
    labels = jnp.searchsorted(jnp.cumsum(tallies), jnp.arange(rows * top), side="right").astype(jnp.int32)
    grid = labels.reshape(top, rows).T
    grid = grid[jax.random.permutation(jax.random.fold_in(own, 1), rows)]
    rotation = jax.random.randint(jax.random.fold_in(own, 2), (rows, 1), 0, top)
    return jnp.take_along_axis(grid, (jnp.arange(top)[None, :] + rotation) % top, axis=1)


def shares(number_of, total, limit, skew, full):
    portions = [(1 << 20) // math.isqrt(rank ** skew) + 1 for rank in range(1, number_of + 1)]
    largest = limit if full else min(limit, max(-(-total // number_of), total * portions[0] // sum(portions)))
    least = 1 if total - largest >= number_of - 1 else 0
    holding, surplus = [largest] + [least] * (number_of - 1), total - largest - least * (number_of - 1)
    while surplus > 0:
        candidates = [i for i in range(1, number_of) if holding[i] < largest] or [i for i in range(1, number_of) if holding[i] < limit]
        mass, remaining = sum([portions[i] for i in candidates]), surplus
        for i in candidates:
            addition = min(limit - holding[i], max(1, remaining * portions[i] // mass), surplus)
            holding[i] = holding[i] + addition
            surplus = surplus - addition
    return np.array(holding)


def scatter_about(key, extent, width, bound, split=(), held_as=jnp.bfloat16):
    entries = jax.random.normal(key, extent, jnp.float32) * width
    if len(split) > 0:
        entries = level_of(key, extent, split, -0.22, 0.18) * entries
    return jnp.clip(entries, min=-bound, max=bound).astype(held_as)


def setup_inputs(seed: int = 0) -> dict:
    seeds = jax.random.split(jax.random.key(seed), 9)
    tokens = scatter_about(seeds[0], (MICRO, TOKENS, D), 1.0, 6.0, ((1, 128),))
    expert_ids_keys = jax.random.split(jax.random.fold_in(seeds[1], 1), MICRO * TOKENS // TOK_DEV)
    expert_ids_turns = jax.random.permutation(jax.random.fold_in(seeds[1], 3), MICRO * TOKENS // TOK_DEV)
    expert_ids = jax.vmap(lambda own, number: deal_out(jax.random.fold_in(seeds[1], 2), own, number, TOK_DEV, EXPERTS, TOPK, SLOTS, 2))(expert_ids_keys, expert_ids_turns).reshape((MICRO, TOKENS, TOPK))
    gate_probs = jnp.clip(jnp.exp(math.log(1.0) - 2.9957323 * jax.random.uniform(seeds[2], (MICRO, TOKENS, TOPK), jnp.float32) ** level_of(seeds[2], (MICRO, TOKENS, TOPK), ((1, 128),), -0.2, 0.2)), 0.05, 1.0)
    capacity = draw_capacity(jax.random.fold_in(seeds[8], 71), 0)
    flows = draw_flows(jax.random.fold_in(seeds[8], 71), 0)
    w_gate = scatter_about(seeds[5], (EXPERTS, D, FF), D ** -0.5, 0.125, ((0, 128),))
    w_up = scatter_about(seeds[6], (EXPERTS, D, FF), D ** -0.5, 0.125, ((0, 128),))
    w_down = scatter_about(seeds[7], (EXPERTS, FF, D), FF ** -0.5, 0.21875, ((0, 128),))
    return {"tokens": tokens, "expert_ids": expert_ids, "gate_probs": gate_probs, "capacity": capacity, "flows": flows, "w_gate": w_gate, "w_up": w_up, "w_down": w_down}


def swiglu_rows(rows_in, gate_mat, up_mat, down_mat):
    gate_val = jnp.dot(rows_in, gate_mat, preferred_element_type=jnp.float32)
    up_val = jnp.dot(rows_in, up_mat, preferred_element_type=jnp.float32)
    hidden = (jax.nn.silu(gate_val) * up_val).astype(jnp.bfloat16)
    return jnp.dot(hidden, down_mat, preferred_element_type=jnp.float32).astype(jnp.bfloat16)


def reference(tokens, expert_ids, gate_probs, capacity, flows, w_gate, w_up, w_down):
    keep_rows = CAP_MAX + PARTNERS * FLOW_MAX
    keep_limit = capacity + jnp.sum(flows, 1)
    expert_iota = jnp.arange(EXPERTS, dtype=jnp.int32)
    results = []
    for micro_index in range(MICRO):
        local_rows = tokens[micro_index]
        pair_expert = expert_ids[micro_index].reshape(-1)
        pair_total = pair_expert.shape[0]
        onehot = (pair_expert[:, None] == expert_iota[None, :]).astype(jnp.int32)
        pair_rank = jnp.sum((jnp.cumsum(onehot, 0) - onehot) * onehot, 1).astype(jnp.int32)
        keep_pair = pair_rank < keep_limit[pair_expert]
        target_row = jnp.where(keep_pair, pair_expert, EXPERTS).astype(jnp.int32)
        probs = gate_probs[micro_index]
        gate_norm = (probs / jnp.sum(probs, 1, keepdims=True)).reshape(-1)
        pair_table = jnp.zeros((EXPERTS, keep_rows), jnp.int32).at[target_row, pair_rank].set(
            jnp.arange(pair_total, dtype=jnp.int32), mode="drop")
        weight_table = jnp.zeros((EXPERTS, keep_rows), gate_norm.dtype).at[target_row, pair_rank].set(
            gate_norm, mode="drop")

        def one_expert(accum_out, packed):
            pair_list, weight_list, gate_mat, up_mat, down_mat = packed
            token_list = pair_list // TOPK
            expert_out = swiglu_rows(local_rows[token_list], gate_mat, up_mat, down_mat)
            added = weight_list[:, None] * expert_out.astype(jnp.float32)
            return accum_out.at[token_list].add(added), None

        accum_out, unused = lax.scan(one_expert, jnp.zeros(local_rows.shape, jnp.float32),
                                     (pair_table, weight_table, w_gate, w_up, w_down))
        results.append(accum_out.astype(jnp.bfloat16))
    return jnp.stack(results)
```

```python
import jax
import jax.numpy as jnp
from jax import lax
from jax.experimental import pallas as pl
from jax.experimental.pallas import tpu as pltpu
from jax.sharding import PartitionSpec as P

AXES = ("expert", "group")
PIECES = 4
MARK = 8.0


def place_of(index, per_device):
    device = jnp.floor((index.astype(jnp.float32) + 0.5) * (1.0 / per_device)).astype(jnp.int32)
    inside = index - device * per_device
    return device, inside // PIECES, inside % PIECES


def ranked(ids, experts):
    tok, top = ids.shape
    lane = lax.broadcasted_iota(jnp.int32, (tok, experts), 1)
    chosen = jnp.zeros((tok, experts), jnp.float32)
    for k in range(top):
        chosen = jnp.where(ids[:, k : k + 1] == lane, 1.0, chosen)
    earlier = lax.broadcasted_iota(jnp.int32, (tok, tok), 0) > lax.broadcasted_iota(jnp.int32, (tok, tok), 1)
    before = jnp.dot(
        jnp.where(earlier, 1.0, 0.0).astype(jnp.bfloat16),
        chosen.astype(jnp.bfloat16),
        preferred_element_type=jnp.float32,
    )
    return chosen * (before + 1.0)


def pack_tokens(tokens, ids, micro, slots, block_devices):
    _, tok, width = tokens.shape
    top = ids.shape[2]
    experts = lax.axis_size(AXES)
    per_device = slots * PIECES
    part = width // PIECES
    rows = block_devices * per_device

    def kernel(ids_ref, tok_ref, out_ref, rank_ref, piece_ref):
        step = pl.program_id(0)

        @pl.when(step == 0)
        def _():
            rank_ref[...] = ranked(ids_ref[0], experts).T.astype(jnp.bfloat16)
            for q in range(PIECES):
                piece_ref[q * tok : (q + 1) * tok, :] = tok_ref[0, :, q * part : (q + 1) * part]

        row = lax.broadcasted_iota(jnp.int32, (rows, experts), 0)
        col = lax.broadcasted_iota(jnp.int32, (rows, experts), 1)
        device, slot, piece = place_of(row, per_device)
        spread = jnp.where(device + step * block_devices == col, 1.0, 0.0).astype(jnp.bfloat16)
        rank = jnp.dot(spread, rank_ref[...], preferred_element_type=jnp.float32)
        hit = jnp.where(rank == (slot + 1).astype(jnp.float32), 1.0, 0.0)
        select = jnp.concatenate(
            [jnp.where(piece == q, hit, 0.0).astype(jnp.bfloat16) for q in range(PIECES)], axis=1
        )
        moved = jnp.dot(select, piece_ref[...], preferred_element_type=jnp.float32)
        filled = jnp.sum(hit, axis=1, keepdims=True)
        mark = jnp.where((filled < 0.5) & (piece == 0) & (col == 0), MARK, 0.0)
        out_ref[:, :experts] = (moved[:, :experts] + mark).astype(jnp.bfloat16)
        out_ref[:, experts:] = moved[:, experts:].astype(jnp.bfloat16)

    return pl.pallas_call(
        kernel,
        grid=(experts // block_devices,),
        in_specs=[
            pl.BlockSpec((1, tok, top), lambda i: (micro, 0, 0)),
            pl.BlockSpec((1, tok, width), lambda i: (micro, 0, 0)),
        ],
        out_specs=pl.BlockSpec((rows, part), lambda i: (i, 0)),
        out_shape=jax.ShapeDtypeStruct((experts * per_device, part), jnp.bfloat16),
        scratch_shapes=[
            pltpu.VMEM((experts, tok), jnp.bfloat16),
            pltpu.VMEM((PIECES * tok, part), jnp.bfloat16),
        ],
        name="pack_tokens",
    )(ids, tokens)


def mix_answers(answered, ids, probs, micro, slots, block_devices, earlier_out):
    micros, tok, top = ids.shape
    experts = lax.axis_size(AXES)
    per_device = slots * PIECES
    part = answered.shape[1]
    width = part * PIECES
    rows = block_devices * per_device
    steps = experts // block_devices

    def kernel(ids_ref, probs_ref, rows_ref, *rest):
        out_ref, rank_ref, gate_ref, sum_ref = rest[-4:]
        step = pl.program_id(0)

        @pl.when(step == 0)
        def _():
            ids_here = ids_ref[0]
            probs_here = probs_ref[0]
            norm = probs_here / jnp.sum(probs_here, axis=1, keepdims=True)
            lane = lax.broadcasted_iota(jnp.int32, (tok, experts), 1)
            gate = jnp.zeros((tok, experts), jnp.float32)
            for k in range(top):
                gate = jnp.where(ids_here[:, k : k + 1] == lane, norm[:, k : k + 1], gate)
            gate_ref[...] = gate.astype(jnp.bfloat16)
            rank_ref[...] = ranked(ids_here, experts).astype(jnp.bfloat16)
            sum_ref[...] = jnp.zeros_like(sum_ref)

        lane = lax.broadcasted_iota(jnp.int32, (experts, rows), 1)
        sub = lax.broadcasted_iota(jnp.int32, (experts, rows), 0)
        device, _, _ = place_of(lane, per_device)
        spread = jnp.where(device + step * block_devices == sub, 1.0, 0.0).astype(jnp.bfloat16)
        rank = jnp.dot(rank_ref[...], spread, preferred_element_type=jnp.float32)
        gate = jnp.dot(gate_ref[...], spread, preferred_element_type=jnp.float32)
        _, slot, piece = place_of(lax.broadcasted_iota(jnp.int32, (tok, rows), 1), per_device)
        weight = jnp.where(rank == (slot + 1).astype(jnp.float32), gate, 0.0)
        weights = jnp.concatenate(
            [jnp.where(piece == q, weight, 0.0).astype(jnp.bfloat16) for q in range(PIECES)], axis=0
        )
        sum_ref[...] += jnp.dot(weights, rows_ref[...], preferred_element_type=jnp.float32)

        @pl.when(step == steps - 1)
        def _():
            for q in range(PIECES):
                out_ref[0, :, q * part : (q + 1) * part] = sum_ref[q * tok : (q + 1) * tok, :].astype(
                    jnp.bfloat16
                )

    in_specs = [
        pl.BlockSpec((1, tok, top), lambda i: (micro, 0, 0)),
        pl.BlockSpec((1, tok, top), lambda i: (micro, 0, 0)),
        pl.BlockSpec((rows, part), lambda i: (i, 0)),
    ]
    operands = [ids, probs, answered]
    aliases = {}
    if earlier_out is not None:
        in_specs.append(pl.BlockSpec(memory_space=pl.ANY))
        operands.append(earlier_out)
        aliases = {3: 0}
    return pl.pallas_call(
        kernel,
        grid=(steps,),
        in_specs=in_specs,
        out_specs=pl.BlockSpec((1, tok, width), lambda i: (micro, 0, 0)),
        out_shape=jax.ShapeDtypeStruct((micros, tok, width), jnp.bfloat16),
        scratch_shapes=[
            pltpu.VMEM((tok, experts), jnp.bfloat16),
            pltpu.VMEM((tok, experts), jnp.bfloat16),
            pltpu.VMEM((PIECES * tok, part), jnp.float32),
        ],
        input_output_aliases=aliases,
        name="mix_answers",
    )(*operands)


def run_expert(arrived, keep_limit, gate_mat, up_mat, down_mat, slots, block_devices):
    packed_rows, part = arrived.shape
    width, hidden_dim = gate_mat.shape[1:]
    turn = 16 * slots
    turns = block_devices * slots // turn
    rows = block_devices * slots
    steps = packed_rows // (rows * PIECES)

    def kernel(limit_ref, in_ref, gate_ref, up_ref, down_ref, out_ref, join_ref, split_ref, rows_ref, seen_ref):
        step = pl.program_id(0)

        @pl.when(step == 0)
        def _():
            seen_ref[...] = jnp.zeros_like(seen_ref)
            for q in range(PIECES):
                row = lax.broadcasted_iota(jnp.int32, (turn, turn * PIECES), 0)
                col = lax.broadcasted_iota(jnp.int32, (turn, turn * PIECES), 1)
                join_ref[q] = jnp.where(col == row * PIECES + q, 1.0, 0.0).astype(jnp.bfloat16)
                row = lax.broadcasted_iota(jnp.int32, (turn * PIECES, turn), 0)
                col = lax.broadcasted_iota(jnp.int32, (turn * PIECES, turn), 1)
                split_ref[q] = jnp.where(row == col * PIECES + q, 1.0, 0.0).astype(jnp.bfloat16)

        for j in range(turns):
            pieces = in_ref[j * turn * PIECES : (j + 1) * turn * PIECES, :]
            for q in range(PIECES):
                rows_ref[j * turn : (j + 1) * turn, q * part : (q + 1) * part] = jnp.dot(
                    join_ref[q], pieces, preferred_element_type=jnp.float32
                ).astype(jnp.bfloat16)
        rows_here = rows_ref[...]
        lanes = seen_ref.shape[1]
        live = jnp.where(
            jnp.broadcast_to(rows_here[:, :1].astype(jnp.float32), (rows, lanes)) < MARK - 1.0, 1.0, 0.0
        )
        above = lax.broadcasted_iota(jnp.int32, (rows, rows), 0) > lax.broadcasted_iota(jnp.int32, (rows, rows), 1)
        rank = seen_ref[...] + jnp.dot(
            jnp.where(above, 1.0, 0.0).astype(jnp.bfloat16),
            live.astype(jnp.bfloat16),
            preferred_element_type=jnp.float32,
        )
        seen_ref[...] += jnp.sum(live, axis=0, keepdims=True)
        limit = limit_ref[0].astype(jnp.float32)
        kept = (live > 0.5) & (rank < limit)
        kept = jnp.where(kept, 1.0, 0.0)[:, :1] > 0.5

        gate_val = jnp.dot(rows_here, gate_ref[0], preferred_element_type=jnp.float32)
        up_val = jnp.dot(rows_here, up_ref[0], preferred_element_type=jnp.float32)
        hidden = (gate_val * lax.logistic(gate_val) * up_val).astype(jnp.bfloat16)
        out_val = jnp.dot(hidden, down_ref[0], preferred_element_type=jnp.float32)
        out_val = jnp.where(kept, out_val, 0.0).astype(jnp.bfloat16)
        for j in range(turns):
            moved = jnp.zeros((turn * PIECES, part), jnp.float32)
            for q in range(PIECES):
                moved = moved + jnp.dot(
                    split_ref[q],
                    out_val[j * turn : (j + 1) * turn, q * part : (q + 1) * part],
                    preferred_element_type=jnp.float32,
                )
            out_ref[j * turn * PIECES : (j + 1) * turn * PIECES, :] = moved.astype(jnp.bfloat16)

    return pl.pallas_call(
        kernel,
        grid=(steps,),
        in_specs=[
            pl.BlockSpec(memory_space=pltpu.SMEM),
            pl.BlockSpec((rows * PIECES, part), lambda i: (i, 0)),
            pl.BlockSpec((1, width, hidden_dim), lambda i: (0, 0, 0)),
            pl.BlockSpec((1, width, hidden_dim), lambda i: (0, 0, 0)),
            pl.BlockSpec((1, hidden_dim, width), lambda i: (0, 0, 0)),
        ],
        out_specs=pl.BlockSpec((rows * PIECES, part), lambda i: (i, 0)),
        out_shape=jax.ShapeDtypeStruct((packed_rows, part), jnp.bfloat16),
        scratch_shapes=[
            pltpu.VMEM((PIECES, turn, turn * PIECES), jnp.bfloat16),
            pltpu.VMEM((PIECES, turn * PIECES, turn), jnp.bfloat16),
            pltpu.VMEM((rows, width), jnp.bfloat16),
            pltpu.VMEM((1, 128), jnp.float32),
        ],
        name="run_expert",
    )(keep_limit, arrived, gate_mat, up_mat, down_mat)


def swap(rows, devices):
    parts = rows.reshape(devices, rows.shape[0] // devices, rows.shape[1])
    return lax.all_to_all(parts, AXES, split_axis=0, concat_axis=0, tiled=True)


def body(tokens, expert_ids, gate_probs, capacity, flows, w_gate, w_up, w_down):
    devices = lax.axis_size(AXES)
    micros, tok, width = tokens.shape
    top = expert_ids.shape[2]
    slots = tok * top * 5 // (4 * devices)
    block_devices = 16
    keep_limit = capacity + jnp.sum(flows, 1)

    arrived = []
    for m in range(micros):
        packed = pack_tokens(tokens, expert_ids, m, slots, block_devices)
        arrived.append(swap(packed, devices))
    answers = []
    for m in range(micros):
        incoming = arrived[m].reshape(-1, width // PIECES)
        returned = run_expert(incoming, keep_limit, w_gate, w_up, w_down, slots, 2 * block_devices)
        answers.append(swap(returned, devices))
    out = None
    for m in range(micros):
        answered = answers[m].reshape(-1, width // PIECES)
        out = mix_answers(answered, expert_ids, gate_probs, m, slots, block_devices, out)
    return out


def solution(mesh):
    placed = (
        P(None, AXES, None),
        P(None, AXES, None),
        P(None, AXES, None),
        P(AXES),
        P(AXES, None),
        P(AXES, None, None),
        P(AXES, None, None),
        P(AXES, None, None),
    )
    return jax.shard_map(
        body,
        mesh=mesh,
        in_specs=placed,
        out_specs=P(None, AXES, None),
        check_vma=False,
    )
```

```python
import jax
import jax.numpy as jnp
from jax import lax
from jax.experimental import pallas as pl
from jax.experimental.pallas import tpu as pltpu
from jax.sharding import PartitionSpec as P

AXES = ("expert", "group")
PIECES = 4
TILE = 8
MARK = 8.0


def iota(shape, dim):
    return lax.broadcasted_iota(jnp.int32, shape, dim)


def bit(condition):
    return jnp.where(condition, 1.0, 0.0)


def narrow(x):
    return x.astype(jnp.bfloat16)


def mm(a, b):
    return jnp.dot(a, b, preferred_element_type=jnp.float32)


def chosen_rank(ids, experts):
    top, tok = ids.shape
    expert = iota((experts, tok), 0)
    chosen = jnp.zeros((experts, tok), jnp.float32)
    for k in range(top):
        chosen = jnp.where(ids[k : k + 1, :] == expert, 1.0, chosen)
    before = mm(narrow(chosen), narrow(bit(iota((tok, tok), 0) < iota((tok, tok), 1))))
    return chosen * (before + 1.0)


def pack_tokens(tokens, ids, micro, block):
    _, tok, width = tokens.shape
    top = ids.shape[1]
    experts = lax.axis_size(AXES)
    part = width // PIECES
    rows = block * TILE

    def kernel(ids_ref, tok_ref, out_ref, rank_ref, piece_ref):
        step = pl.program_id(0)

        @pl.when(step == 0)
        def _():
            rank_ref[...] = narrow(chosen_rank(ids_ref[0], experts))
            for q in range(PIECES):
                piece_ref[q * tok : (q + 1) * tok, :] = tok_ref[0, :, q * part : (q + 1) * part]

        row = iota((rows, experts), 0)
        col = iota((rows, experts), 1)
        spread = narrow(bit((row >> 3) + step * block == col))
        rank = mm(spread, rank_ref[...])
        inside = row & 7
        hit = bit(rank == (inside + 1).astype(jnp.float32))
        select = narrow(hit)
        first = col == 0
        mark = jnp.where((jnp.sum(hit, axis=1, keepdims=True) < 0.5) & first, MARK, 0.0)
        for q in range(PIECES):
            moved = mm(select, piece_ref[q * tok : (q + 1) * tok, :])
            if q == 0:
                moved = jnp.concatenate([moved[:, :experts] + mark, moved[:, experts:]], axis=1)
            out_ref[:, q] = narrow(moved.reshape(block, TILE, part))
        hit = bit(rank == ((inside >> 2) + (TILE + 1)).astype(jnp.float32))
        piece = inside & 3
        select = jnp.concatenate([narrow(jnp.where(piece == q, hit, 0.0)) for q in range(PIECES)], axis=1)
        moved = mm(select, piece_ref[...])
        mark = jnp.where((jnp.sum(hit, axis=1, keepdims=True) < 0.5) & first & (piece == 0), MARK, 0.0)
        moved = jnp.concatenate([moved[:, :experts] + mark, moved[:, experts:]], axis=1)
        out_ref[:, PIECES] = narrow(moved.reshape(block, TILE, part))

    shape = (PIECES + 1, TILE, part)
    return pl.pallas_call(
        kernel,
        grid=(experts // block,),
        in_specs=[
            pl.BlockSpec((1, top, tok), lambda i: (micro, 0, 0)),
            pl.BlockSpec((1, tok, width), lambda i: (micro, 0, 0)),
        ],
        out_specs=pl.BlockSpec((block, *shape), lambda i: (i, 0, 0, 0)),
        out_shape=jax.ShapeDtypeStruct((experts, *shape), jnp.bfloat16),
        scratch_shapes=[
            pltpu.VMEM((experts, tok), jnp.bfloat16),
            pltpu.VMEM((PIECES * tok, part), jnp.bfloat16),
        ],
        name="pack_tokens",
    )(ids, tokens)


def mix_answers(answered, ids, probs, micro, block, earlier_out):
    micros, top, tok = ids.shape
    experts = lax.axis_size(AXES)
    part = answered.shape[3]
    width = part * PIECES
    rows = block * TILE
    steps = experts // block

    def kernel(ids_ref, probs_ref, rows_ref, *rest):
        out_ref, rank_ref, gate_ref, sum_ref = rest[-4:]
        step = pl.program_id(0)

        @pl.when(step == 0)
        def _():
            ids_here = ids_ref[0]
            probs_here = probs_ref[0]
            norm = probs_here / jnp.sum(probs_here, axis=0, keepdims=True)
            expert = iota((experts, tok), 0)
            gate = jnp.zeros((experts, tok), jnp.float32)
            for k in range(top):
                gate = jnp.where(ids_here[k : k + 1, :] == expert, norm[k : k + 1, :], gate)
            gate_ref[...] = narrow(gate.T)
            rank_ref[...] = narrow(chosen_rank(ids_here, experts).T)
            sum_ref[...] = jnp.zeros_like(sum_ref)

        col = iota((experts, rows), 1)
        spread = narrow(bit((col >> 3) + step * block == iota((experts, rows), 0)))
        rank = mm(rank_ref[...], spread)
        gate = mm(gate_ref[...], spread)
        inside = iota((tok, rows), 1) & 7
        weight = narrow(jnp.where(rank == (inside + 1).astype(jnp.float32), gate, 0.0))
        rest_weight = jnp.where(rank == ((inside >> 2) + (TILE + 1)).astype(jnp.float32), gate, 0.0)
        last = rows_ref[:, PIECES].reshape(rows, part)
        for q in range(PIECES):
            mine = narrow(jnp.where((inside & 3) == q, rest_weight, 0.0))
            both = jnp.concatenate([weight, mine], axis=1)
            values = jnp.concatenate([rows_ref[:, q].reshape(rows, part), last], axis=0)
            sum_ref[:, q * part : (q + 1) * part] += mm(both, values)

        @pl.when(step == steps - 1)
        def _():
            out_ref[0] = narrow(sum_ref[...])

    in_specs = [
        pl.BlockSpec((1, top, tok), lambda i: (micro, 0, 0)),
        pl.BlockSpec((1, top, tok), lambda i: (micro, 0, 0)),
        pl.BlockSpec((block, PIECES + 1, TILE, part), lambda i: (i, 0, 0, 0)),
    ]
    operands = [ids, probs, answered]
    aliases = {}
    if earlier_out is not None:
        in_specs.append(pl.BlockSpec(memory_space=pl.ANY))
        operands.append(earlier_out)
        aliases = {3: 0}
    return pl.pallas_call(
        kernel,
        grid=(steps,),
        in_specs=in_specs,
        out_specs=pl.BlockSpec((1, tok, width), lambda i: (micro, 0, 0)),
        out_shape=jax.ShapeDtypeStruct((micros, tok, width), jnp.bfloat16),
        scratch_shapes=[
            pltpu.VMEM((tok, experts), jnp.bfloat16),
            pltpu.VMEM((tok, experts), jnp.bfloat16),
            pltpu.VMEM((tok, width), jnp.float32),
        ],
        input_output_aliases=aliases,
        name="mix_answers",
    )(*operands)


def place(row, slots, q):
    device = jnp.floor((row.astype(jnp.float32) + 0.5) * (1.0 / slots)).astype(jnp.int32)
    slot = row - device * slots
    inside = jnp.where(slot < TILE, q * TILE + slot, slot * PIECES + q)
    return device * slots * PIECES + inside


def run_expert(arrived, keep_limit, gate_mat, up_mat, down_mat, slots, block_devices):
    packed_rows, part = arrived.shape
    width, hidden_dim = gate_mat.shape[1:]
    turn = 16 * slots
    turns = block_devices * slots // turn
    rows = block_devices * slots
    steps = packed_rows // (rows * PIECES)

    def kernel(limit_ref, in_ref, gate_ref, up_ref, down_ref, out_ref, join_ref, split_ref, rows_ref, seen_ref):
        step = pl.program_id(0)

        @pl.when(step == 0)
        def _():
            seen_ref[...] = jnp.zeros_like(seen_ref)
            for q in range(PIECES):
                shape = (turn, turn * PIECES)
                join_ref[q] = narrow(bit(place(iota(shape, 0), slots, q) == iota(shape, 1)))
                shape = (turn * PIECES, turn)
                split_ref[q] = narrow(bit(place(iota(shape, 1), slots, q) == iota(shape, 0)))

        for j in range(turns):
            pieces = in_ref[j * turn * PIECES : (j + 1) * turn * PIECES, :]
            for q in range(PIECES):
                rows_ref[j * turn : (j + 1) * turn, q * part : (q + 1) * part] = jnp.dot(
                    join_ref[q], pieces, preferred_element_type=jnp.float32
                ).astype(jnp.bfloat16)
        rows_here = rows_ref[...]
        lanes = seen_ref.shape[1]
        live = jnp.where(
            jnp.broadcast_to(rows_here[:, :1].astype(jnp.float32), (rows, lanes)) < MARK - 1.0, 1.0, 0.0
        )
        above = lax.broadcasted_iota(jnp.int32, (rows, rows), 0) > lax.broadcasted_iota(jnp.int32, (rows, rows), 1)
        rank = seen_ref[...] + jnp.dot(
            jnp.where(above, 1.0, 0.0).astype(jnp.bfloat16),
            live.astype(jnp.bfloat16),
            preferred_element_type=jnp.float32,
        )
        seen_ref[...] += jnp.sum(live, axis=0, keepdims=True)
        limit = limit_ref[0].astype(jnp.float32)
        kept = (live > 0.5) & (rank < limit)
        kept = jnp.where(kept, 1.0, 0.0)[:, :1] > 0.5

        gate_val = jnp.dot(rows_here, gate_ref[0], preferred_element_type=jnp.float32)
        up_val = jnp.dot(rows_here, up_ref[0], preferred_element_type=jnp.float32)
        hidden = (gate_val * lax.logistic(gate_val) * up_val).astype(jnp.bfloat16)
        out_val = jnp.dot(hidden, down_ref[0], preferred_element_type=jnp.float32)
        out_val = jnp.where(kept, out_val, 0.0).astype(jnp.bfloat16)
        for j in range(turns):
            moved = jnp.zeros((turn * PIECES, part), jnp.float32)
            for q in range(PIECES):
                moved = moved + jnp.dot(
                    split_ref[q],
                    out_val[j * turn : (j + 1) * turn, q * part : (q + 1) * part],
                    preferred_element_type=jnp.float32,
                )
            out_ref[j * turn * PIECES : (j + 1) * turn * PIECES, :] = moved.astype(jnp.bfloat16)

    return pl.pallas_call(
        kernel,
        grid=(steps,),
        in_specs=[
            pl.BlockSpec(memory_space=pltpu.SMEM),
            pl.BlockSpec((rows * PIECES, part), lambda i: (i, 0)),
            pl.BlockSpec((1, width, hidden_dim), lambda i: (0, 0, 0)),
            pl.BlockSpec((1, width, hidden_dim), lambda i: (0, 0, 0)),
            pl.BlockSpec((1, hidden_dim, width), lambda i: (0, 0, 0)),
        ],
        out_specs=pl.BlockSpec((rows * PIECES, part), lambda i: (i, 0)),
        out_shape=jax.ShapeDtypeStruct((packed_rows, part), jnp.bfloat16),
        scratch_shapes=[
            pltpu.VMEM((PIECES, turn, turn * PIECES), jnp.bfloat16),
            pltpu.VMEM((PIECES, turn * PIECES, turn), jnp.bfloat16),
            pltpu.VMEM((rows, width), jnp.bfloat16),
            pltpu.VMEM((1, 128), jnp.float32),
        ],
        name="run_expert",
    )(keep_limit, arrived, gate_mat, up_mat, down_mat)


def swap(rows, devices):
    parts = rows.reshape(devices, -1, rows.shape[-1])
    return lax.all_to_all(parts, AXES, split_axis=0, concat_axis=0, tiled=True)


def body(tokens, expert_ids, gate_probs, capacity, flows, w_gate, w_up, w_down):
    devices = lax.axis_size(AXES)
    micros, tok, width = tokens.shape
    top = expert_ids.shape[2]
    ids = jnp.swapaxes(expert_ids, 1, 2)
    probs = jnp.swapaxes(gate_probs, 1, 2)
    slots = tok * top * 5 // (4 * devices)
    block_devices = 64
    keep_limit = capacity + jnp.sum(flows, 1)

    arrived = []
    for m in range(micros):
        packed = pack_tokens(tokens, ids, m, block_devices)
        arrived.append(swap(packed, devices))
    answers = []
    for m in range(micros):
        incoming = arrived[m].reshape(-1, width // PIECES)
        returned = run_expert(incoming, keep_limit, w_gate, w_up, w_down, slots, block_devices // 2)
        answers.append(swap(returned, devices))
    out = None
    for m in range(micros):
        answered = answers[m].reshape(devices, PIECES + 1, TILE, width // PIECES)
        out = mix_answers(answered, ids, probs, m, block_devices, out)
    return out


def solution(mesh):
    placed = (
        P(None, AXES, None),
        P(None, AXES, None),
        P(None, AXES, None),
        P(AXES),
        P(AXES, None),
        P(AXES, None, None),
        P(AXES, None, None),
        P(AXES, None, None),
    )
    return jax.shard_map(
        body,
        mesh=mesh,
        in_specs=placed,
        out_specs=P(None, AXES, None),
        check_vma=False,
    )
```

```python
import jax
import jax.numpy as jnp
from jax import lax
from jax.experimental import pallas as pl
from jax.experimental.pallas import tpu as pltpu
from jax.sharding import PartitionSpec as P

AXES = ("expert", "group")
PIECES = 4
TILE = 8
MARK = 8.0


def iota(shape, dim):
    return lax.broadcasted_iota(jnp.int32, shape, dim)


def bit(condition):
    return jnp.where(condition, 1.0, 0.0)


def narrow(x):
    return x.astype(jnp.bfloat16)


def mm(a, b):
    return jnp.dot(a, b, preferred_element_type=jnp.float32)


def chosen_rank(ids, experts):
    top, tok = ids.shape
    expert = iota((experts, tok), 0)
    chosen = jnp.zeros((experts, tok), jnp.float32)
    for k in range(top):
        chosen = jnp.where(ids[k : k + 1, :] == expert, 1.0, chosen)
    before = mm(narrow(chosen), narrow(bit(iota((tok, tok), 0) < iota((tok, tok), 1))))
    return chosen * (before + 1.0)


def pack_tokens(tokens, ids, micro):
    _, tok, width = tokens.shape
    top = ids.shape[1]
    experts = lax.axis_size(AXES)
    part = width // PIECES
    rows = experts * TILE

    def kernel(ids_ref, tok_ref, out_ref, sent_ref, my_ids_ref, my_tok_ref, sems):
        def leave(q):
            return pltpu.make_async_copy(sent_ref.at[q], out_ref.at[:, q], sems.at[q])

        get_ids = pltpu.make_async_copy(ids_ref.at[micro], my_ids_ref, sems.at[PIECES + 1])
        get_ids.start()

        get_tokens = pltpu.make_async_copy(tok_ref.at[micro], my_tok_ref, sems.at[PIECES + 2])
        get_tokens.start()
        get_ids.wait()
        order = narrow(chosen_rank(my_ids_ref[...], experts))
        row = iota((rows, experts), 0)
        col = iota((rows, experts), 1)
        rank = mm(narrow(bit((row >> 3) == col)), order)
        inside = row & 7
        hit = bit(rank == (inside + 1).astype(jnp.float32))
        select = narrow(hit)
        first = col == 0
        mark = jnp.where((jnp.sum(hit, axis=1, keepdims=True) < 0.5) & first, MARK, 0.0)
        get_tokens.wait()
        for q in range(PIECES):
            moved = mm(select, my_tok_ref[:, q * part : (q + 1) * part])
            if q == 0:
                moved = jnp.concatenate([moved[:, :experts] + mark, moved[:, experts:]], axis=1)
            sent_ref[q] = narrow(moved.reshape(experts, TILE, part))
            leave(q).start()
        hit = bit(rank == ((inside >> 2) + (TILE + 1)).astype(jnp.float32))
        piece = inside & 3
        select = jnp.concatenate([narrow(jnp.where(piece == q, hit, 0.0)) for q in range(PIECES)], axis=1)
        stacked = jnp.concatenate([my_tok_ref[:, q * part : (q + 1) * part] for q in range(PIECES)], axis=0)
        moved = mm(select, stacked)
        mark = jnp.where((jnp.sum(hit, axis=1, keepdims=True) < 0.5) & first & (piece == 0), MARK, 0.0)
        moved = jnp.concatenate([moved[:, :experts] + mark, moved[:, experts:]], axis=1)
        sent_ref[PIECES] = narrow(moved.reshape(experts, TILE, part))
        leave(PIECES).start()
        for q in range(PIECES + 1):
            leave(q).wait()

    return pl.pallas_call(
        kernel,
        grid=(1,),
        in_specs=[pl.BlockSpec(memory_space=pl.ANY)] * 2,
        out_specs=pl.BlockSpec(memory_space=pl.ANY),
        out_shape=jax.ShapeDtypeStruct((experts, PIECES + 1, TILE, part), jnp.bfloat16),
        scratch_shapes=[
            pltpu.VMEM((PIECES + 1, experts, TILE, part), jnp.bfloat16),
            pltpu.VMEM((top, tok), ids.dtype),
            pltpu.VMEM((tok, width), jnp.bfloat16),
            pltpu.SemaphoreType.DMA((PIECES + 3,)),
        ],
        name="pack_tokens",
    )(ids, tokens)


def mix_answers(answered, ids, probs, micro, earlier_out):
    micros, top, tok = ids.shape
    experts = lax.axis_size(AXES)
    part = answered.shape[3]
    width = part * PIECES
    rows = experts * TILE

    def kernel(ids_ref, probs_ref, rows_ref, *rest):
        out_ref, here_ref, my_ids_ref, my_probs_ref, sems = rest[-5:]

        def fetch(q):
            return pltpu.make_async_copy(rows_ref.at[:, q], here_ref.at[q], sems.at[q])

        get_ids = pltpu.make_async_copy(ids_ref.at[micro], my_ids_ref, sems.at[PIECES + 1])
        get_probs = pltpu.make_async_copy(probs_ref.at[micro], my_probs_ref, sems.at[PIECES + 2])
        get_ids.start()
        get_probs.start()
        for q in (PIECES, *range(PIECES)):
            fetch(q).start()
        get_ids.wait()
        get_probs.wait()
        ids_here = my_ids_ref[...]
        probs_here = my_probs_ref[...]
        norm = probs_here / jnp.sum(probs_here, axis=0, keepdims=True)
        expert = iota((experts, tok), 0)
        gate = jnp.zeros((experts, tok), jnp.float32)
        for k in range(top):
            gate = jnp.where(ids_here[k : k + 1, :] == expert, norm[k : k + 1, :], gate)
        spread = narrow(bit((iota((experts, rows), 1) >> 3) == iota((experts, rows), 0)))
        rank = mm(narrow(chosen_rank(ids_here, experts).T), spread)
        gate = mm(narrow(gate.T), spread)
        inside = iota((tok, rows), 1) & 7
        weight = narrow(jnp.where(rank == (inside + 1).astype(jnp.float32), gate, 0.0))
        rest_weight = jnp.where(rank == ((inside >> 2) + (TILE + 1)).astype(jnp.float32), gate, 0.0)
        rest_weight = jnp.concatenate(
            [narrow(jnp.where((inside & 3) == q, rest_weight, 0.0)) for q in range(PIECES)], axis=0
        )
        fetch(PIECES).wait()
        last = mm(rest_weight, here_ref[PIECES].reshape(rows, part))
        for q in range(PIECES):
            fetch(q).wait()
            main = mm(weight, here_ref[q].reshape(rows, part))
            out_ref[0, :, q * part : (q + 1) * part] = narrow(main + last[q * tok : (q + 1) * tok])

    in_specs = [pl.BlockSpec(memory_space=pl.ANY)] * 3
    operands = [ids, probs, answered]
    aliases = {}
    if earlier_out is not None:
        in_specs.append(pl.BlockSpec(memory_space=pl.ANY))
        operands.append(earlier_out)
        aliases = {3: 0}
    return pl.pallas_call(
        kernel,
        grid=(1,),
        in_specs=in_specs,
        out_specs=pl.BlockSpec((1, tok, width), lambda i: (micro, 0, 0)),
        out_shape=jax.ShapeDtypeStruct((micros, tok, width), jnp.bfloat16),
        scratch_shapes=[
            pltpu.VMEM((PIECES + 1, experts, TILE, part), jnp.bfloat16),
            pltpu.VMEM((top, tok), ids.dtype),
            pltpu.VMEM((top, tok), probs.dtype),
            pltpu.SemaphoreType.DMA((PIECES + 3,)),
        ],
        input_output_aliases=aliases,
        name="mix_answers",
    )(*operands)


def place(row, slots, q):
    device = jnp.floor((row.astype(jnp.float32) + 0.5) * (1.0 / slots)).astype(jnp.int32)
    slot = row - device * slots
    inside = jnp.where(slot < TILE, q * TILE + slot, slot * PIECES + q)
    return device * slots * PIECES + inside


def run_expert(arrived, keep_limit, gate_mat, up_mat, down_mat, slots, block_devices):
    packed_rows, part = arrived.shape
    width, hidden_dim = gate_mat.shape[1:]
    turn = 16 * slots
    turns = block_devices * slots // turn
    rows = block_devices * slots
    steps = packed_rows // (rows * PIECES)

    def kernel(limit_ref, in_ref, gate_ref, up_ref, down_ref, out_ref, join_ref, split_ref, rows_ref, seen_ref):
        step = pl.program_id(0)

        @pl.when(step == 0)
        def _():
            seen_ref[...] = jnp.zeros_like(seen_ref)
            for q in range(PIECES):
                shape = (turn, turn * PIECES)
                join_ref[q] = narrow(bit(place(iota(shape, 0), slots, q) == iota(shape, 1)))
                shape = (turn * PIECES, turn)
                split_ref[q] = narrow(bit(place(iota(shape, 1), slots, q) == iota(shape, 0)))

        for j in range(turns):
            pieces = in_ref[j * turn * PIECES : (j + 1) * turn * PIECES, :]
            for q in range(PIECES):
                rows_ref[j * turn : (j + 1) * turn, q * part : (q + 1) * part] = jnp.dot(
                    join_ref[q], pieces, preferred_element_type=jnp.float32
                ).astype(jnp.bfloat16)
        rows_here = rows_ref[...]
        lanes = seen_ref.shape[1]
        live = jnp.where(
            jnp.broadcast_to(rows_here[:, :1].astype(jnp.float32), (rows, lanes)) < MARK - 1.0, 1.0, 0.0
        )
        above = lax.broadcasted_iota(jnp.int32, (rows, rows), 0) > lax.broadcasted_iota(jnp.int32, (rows, rows), 1)
        rank = seen_ref[...] + jnp.dot(
            jnp.where(above, 1.0, 0.0).astype(jnp.bfloat16),
            live.astype(jnp.bfloat16),
            preferred_element_type=jnp.float32,
        )
        seen_ref[...] += jnp.sum(live, axis=0, keepdims=True)
        limit = limit_ref[0].astype(jnp.float32)
        kept = (live > 0.5) & (rank < limit)
        kept = jnp.where(kept, 1.0, 0.0)[:, :1] > 0.5

        gate_val = jnp.dot(rows_here, gate_ref[0], preferred_element_type=jnp.float32)
        up_val = jnp.dot(rows_here, up_ref[0], preferred_element_type=jnp.float32)
        hidden = (gate_val * lax.logistic(gate_val) * up_val).astype(jnp.bfloat16)
        out_val = jnp.dot(hidden, down_ref[0], preferred_element_type=jnp.float32)
        out_val = jnp.where(kept, out_val, 0.0).astype(jnp.bfloat16)
        for j in range(turns):
            moved = jnp.zeros((turn * PIECES, part), jnp.float32)
            for q in range(PIECES):
                moved = moved + jnp.dot(
                    split_ref[q],
                    out_val[j * turn : (j + 1) * turn, q * part : (q + 1) * part],
                    preferred_element_type=jnp.float32,
                )
            out_ref[j * turn * PIECES : (j + 1) * turn * PIECES, :] = moved.astype(jnp.bfloat16)

    return pl.pallas_call(
        kernel,
        grid=(steps,),
        in_specs=[
            pl.BlockSpec(memory_space=pltpu.SMEM),
            pl.BlockSpec((rows * PIECES, part), lambda i: (i, 0)),
            pl.BlockSpec((1, width, hidden_dim), lambda i: (0, 0, 0)),
            pl.BlockSpec((1, width, hidden_dim), lambda i: (0, 0, 0)),
            pl.BlockSpec((1, hidden_dim, width), lambda i: (0, 0, 0)),
        ],
        out_specs=pl.BlockSpec((rows * PIECES, part), lambda i: (i, 0)),
        out_shape=jax.ShapeDtypeStruct((packed_rows, part), jnp.bfloat16),
        scratch_shapes=[
            pltpu.VMEM((PIECES, turn, turn * PIECES), jnp.bfloat16),
            pltpu.VMEM((PIECES, turn * PIECES, turn), jnp.bfloat16),
            pltpu.VMEM((rows, width), jnp.bfloat16),
            pltpu.VMEM((1, 128), jnp.float32),
        ],
        name="run_expert",
    )(keep_limit, arrived, gate_mat, up_mat, down_mat)


def swap(rows, devices):
    parts = rows.reshape(devices, -1, rows.shape[-1])
    return lax.all_to_all(parts, AXES, split_axis=0, concat_axis=0, tiled=True)


def body(tokens, expert_ids, gate_probs, capacity, flows, w_gate, w_up, w_down):
    devices = lax.axis_size(AXES)
    micros, tok, width = tokens.shape
    top = expert_ids.shape[2]
    ids = jnp.swapaxes(expert_ids, 1, 2)
    probs = jnp.swapaxes(gate_probs, 1, 2)
    slots = tok * top * 5 // (4 * devices)
    block_devices = 32
    keep_limit = capacity + jnp.sum(flows, 1)

    arrived = []
    for m in range(micros):
        packed = pack_tokens(tokens, ids, m)
        arrived.append(swap(packed, devices))
    answers = []
    for m in range(micros):
        incoming = arrived[m].reshape(-1, width // PIECES)
        returned = run_expert(incoming, keep_limit, w_gate, w_up, w_down, slots, block_devices)
        answers.append(swap(returned, devices))
    out = None
    for m in range(micros):
        answered = answers[m].reshape(devices, PIECES + 1, TILE, width // PIECES)
        out = mix_answers(answered, ids, probs, m, out)
    return out


def solution(mesh):
    placed = (
        P(None, AXES, None),
        P(None, AXES, None),
        P(None, AXES, None),
        P(AXES),
        P(AXES, None),
        P(AXES, None, None),
        P(AXES, None, None),
        P(AXES, None, None),
    )
    return jax.shard_map(
        body,
        mesh=mesh,
        in_specs=placed,
        out_specs=P(None, AXES, None),
        check_vma=False,
    )
```

```python
import jax
import jax.numpy as jnp
from jax import lax
from jax.experimental import pallas as pl
from jax.experimental.pallas import tpu as pltpu
from jax.sharding import PartitionSpec as P

AXES = ("expert", "group")
PIECES = 4
TILE = 8
MARK = 8.0


def iota(shape, dim):
    return lax.broadcasted_iota(jnp.int32, shape, dim)


def bit(condition):
    return jnp.where(condition, 1.0, 0.0)


def narrow(x):
    return x.astype(jnp.bfloat16)


def mm(a, b):
    return jnp.dot(a, b, preferred_element_type=jnp.float32)


def chosen_rank(ids, experts):
    top, tok = ids.shape
    expert = iota((experts, tok), 0)
    chosen = jnp.zeros((experts, tok), jnp.float32)
    for k in range(top):
        chosen = jnp.where(ids[k : k + 1, :] == expert, 1.0, chosen)
    before = mm(narrow(chosen), narrow(bit(iota((tok, tok), 0) < iota((tok, tok), 1))))
    return chosen * (before + 1.0)


def pack_tokens(tokens, ids, micro):
    _, tok, width = tokens.shape
    top = ids.shape[1]
    experts = lax.axis_size(AXES)
    part = width // PIECES
    rows = experts * TILE

    def kernel(ids_ref, tok_ref, out_ref, sent_ref, my_ids_ref, my_tok_ref, sems):
        def leave(q):
            return pltpu.make_async_copy(sent_ref.at[q], out_ref.at[:, q], sems.at[q])

        get_ids = pltpu.make_async_copy(ids_ref.at[micro], my_ids_ref, sems.at[PIECES + 1])
        get_ids.start()

        get_tokens = pltpu.make_async_copy(tok_ref.at[micro], my_tok_ref, sems.at[PIECES + 2])
        get_tokens.start()
        get_ids.wait()
        order = narrow(chosen_rank(my_ids_ref[...], experts))
        row = iota((rows, experts), 0)
        col = iota((rows, experts), 1)
        rank = mm(narrow(bit((row >> 3) == col)), order)
        inside = row & 7
        hit = bit(rank == (inside + 1).astype(jnp.float32))
        select = narrow(hit)
        first = col == 0
        mark = jnp.where((jnp.sum(hit, axis=1, keepdims=True) < 0.5) & first, MARK, 0.0)
        get_tokens.wait()
        for q in range(PIECES):
            moved = mm(select, my_tok_ref[:, q * part : (q + 1) * part])
            if q == 0:
                moved = jnp.concatenate([moved[:, :experts] + mark, moved[:, experts:]], axis=1)
            sent_ref[q] = narrow(moved.reshape(experts, TILE, part))
            leave(q).start()
        hit = bit(rank == ((inside >> 2) + (TILE + 1)).astype(jnp.float32))
        piece = inside & 3
        select = jnp.concatenate([narrow(jnp.where(piece == q, hit, 0.0)) for q in range(PIECES)], axis=1)
        stacked = jnp.concatenate([my_tok_ref[:, q * part : (q + 1) * part] for q in range(PIECES)], axis=0)
        moved = mm(select, stacked)
        mark = jnp.where((jnp.sum(hit, axis=1, keepdims=True) < 0.5) & first & (piece == 0), MARK, 0.0)
        moved = jnp.concatenate([moved[:, :experts] + mark, moved[:, experts:]], axis=1)
        sent_ref[PIECES] = narrow(moved.reshape(experts, TILE, part))
        leave(PIECES).start()
        for q in range(PIECES + 1):
            leave(q).wait()

    return pl.pallas_call(
        kernel,
        grid=(1,),
        in_specs=[pl.BlockSpec(memory_space=pl.ANY)] * 2,
        out_specs=pl.BlockSpec(memory_space=pl.ANY),
        out_shape=jax.ShapeDtypeStruct((experts, PIECES + 1, TILE, part), jnp.bfloat16),
        scratch_shapes=[
            pltpu.VMEM((PIECES + 1, experts, TILE, part), jnp.bfloat16),
            pltpu.VMEM((top, tok), ids.dtype),
            pltpu.VMEM((tok, width), jnp.bfloat16),
            pltpu.SemaphoreType.DMA((PIECES + 3,)),
        ],
        name="pack_tokens",
    )(ids, tokens)


def mix_answers(answered, ids, probs):
    micros, top, tok = ids.shape
    experts = lax.axis_size(AXES)
    part = answered[0].shape[3]
    width = part * PIECES
    rows = experts * TILE

    def kernel(ids_ref, probs_ref, *rest):
        rows_refs = rest[:micros]
        out_ref, here_ref, sems = rest[micros:]

        def fetch(m, q):
            return pltpu.make_async_copy(rows_refs[m].at[:, q], here_ref.at[m, q], sems.at[m, q])

        for m in range(micros):
            for q in (PIECES, *range(PIECES)):
                fetch(m, q).start()
        expert = iota((experts, tok), 0)
        spread = narrow(bit((iota((experts, rows), 1) >> 3) == iota((experts, rows), 0)))
        inside = iota((tok, rows), 1) & 7
        for m in range(micros):
            ids_here = ids_ref[m]
            norm = probs_ref[m] / jnp.sum(probs_ref[m], axis=0, keepdims=True)
            gate = jnp.zeros((experts, tok), jnp.float32)
            for k in range(top):
                gate = jnp.where(ids_here[k : k + 1, :] == expert, norm[k : k + 1, :], gate)
            rank = mm(narrow(chosen_rank(ids_here, experts).T), spread)
            gate = mm(narrow(gate.T), spread)
            weight = narrow(jnp.where(rank == (inside + 1).astype(jnp.float32), gate, 0.0))
            rest_weight = jnp.where(rank == ((inside >> 2) + (TILE + 1)).astype(jnp.float32), gate, 0.0)
            rest_weight = jnp.concatenate(
                [narrow(jnp.where((inside & 3) == q, rest_weight, 0.0)) for q in range(PIECES)], axis=0
            )
            fetch(m, PIECES).wait()
            last = mm(rest_weight, here_ref[m, PIECES].reshape(rows, part))
            for q in range(PIECES):
                fetch(m, q).wait()
                main = mm(weight, here_ref[m, q].reshape(rows, part))
                out_ref[m, :, q * part : (q + 1) * part] = narrow(main + last[q * tok : (q + 1) * tok])

    whole = pl.BlockSpec((micros, top, tok), lambda i: (0, 0, 0))
    return pl.pallas_call(
        kernel,
        grid=(1,),
        in_specs=[whole, whole] + [pl.BlockSpec(memory_space=pl.ANY)] * micros,
        out_specs=pl.BlockSpec((micros, tok, width), lambda i: (0, 0, 0)),
        out_shape=jax.ShapeDtypeStruct((micros, tok, width), jnp.bfloat16),
        scratch_shapes=[
            pltpu.VMEM((micros, PIECES + 1, experts, TILE, part), jnp.bfloat16),
            pltpu.SemaphoreType.DMA((micros, PIECES + 1)),
        ],
        name="mix_answers",
    )(ids, probs, *answered)


def place(row, slots, q):
    device = jnp.floor((row.astype(jnp.float32) + 0.5) * (1.0 / slots)).astype(jnp.int32)
    slot = row - device * slots
    inside = jnp.where(slot < TILE, q * TILE + slot, slot * PIECES + q)
    return device * slots * PIECES + inside


def run_expert(arrived, keep_limit, gate_mat, up_mat, down_mat, slots, block_devices):
    packed_rows, part = arrived.shape
    width, hidden_dim = gate_mat.shape[1:]
    turn = 16 * slots
    turns = block_devices * slots // turn
    rows = block_devices * slots
    steps = packed_rows // (rows * PIECES)

    def kernel(limit_ref, in_ref, gate_ref, up_ref, down_ref, out_ref, join_ref, split_ref, rows_ref, seen_ref):
        step = pl.program_id(0)

        @pl.when(step == 0)
        def _():
            seen_ref[...] = jnp.zeros_like(seen_ref)
            for q in range(PIECES):
                shape = (turn, turn * PIECES)
                join_ref[q] = narrow(bit(place(iota(shape, 0), slots, q) == iota(shape, 1)))
                shape = (turn * PIECES, turn)
                split_ref[q] = narrow(bit(place(iota(shape, 1), slots, q) == iota(shape, 0)))

        for j in range(turns):
            pieces = in_ref[j * turn * PIECES : (j + 1) * turn * PIECES, :]
            for q in range(PIECES):
                rows_ref[j * turn : (j + 1) * turn, q * part : (q + 1) * part] = jnp.dot(
                    join_ref[q], pieces, preferred_element_type=jnp.float32
                ).astype(jnp.bfloat16)
        rows_here = rows_ref[...]
        lanes = seen_ref.shape[1]
        live = jnp.where(
            jnp.broadcast_to(rows_here[:, :1].astype(jnp.float32), (rows, lanes)) < MARK - 1.0, 1.0, 0.0
        )
        above = lax.broadcasted_iota(jnp.int32, (rows, rows), 0) > lax.broadcasted_iota(jnp.int32, (rows, rows), 1)
        rank = seen_ref[...] + jnp.dot(
            jnp.where(above, 1.0, 0.0).astype(jnp.bfloat16),
            live.astype(jnp.bfloat16),
            preferred_element_type=jnp.float32,
        )
        seen_ref[...] += jnp.sum(live, axis=0, keepdims=True)
        limit = limit_ref[0].astype(jnp.float32)
        kept = (live > 0.5) & (rank < limit)
        kept = jnp.where(kept, 1.0, 0.0)[:, :1] > 0.5

        gate_val = jnp.dot(rows_here, gate_ref[0], preferred_element_type=jnp.float32)
        up_val = jnp.dot(rows_here, up_ref[0], preferred_element_type=jnp.float32)
        hidden = (gate_val * lax.logistic(gate_val) * up_val).astype(jnp.bfloat16)
        out_val = jnp.dot(hidden, down_ref[0], preferred_element_type=jnp.float32)
        out_val = jnp.where(kept, out_val, 0.0).astype(jnp.bfloat16)
        for j in range(turns):
            moved = jnp.zeros((turn * PIECES, part), jnp.float32)
            for q in range(PIECES):
                moved = moved + jnp.dot(
                    split_ref[q],
                    out_val[j * turn : (j + 1) * turn, q * part : (q + 1) * part],
                    preferred_element_type=jnp.float32,
                )
            out_ref[j * turn * PIECES : (j + 1) * turn * PIECES, :] = moved.astype(jnp.bfloat16)

    return pl.pallas_call(
        kernel,
        grid=(steps,),
        in_specs=[
            pl.BlockSpec(memory_space=pltpu.SMEM),
            pl.BlockSpec((rows * PIECES, part), lambda i: (i, 0)),
            pl.BlockSpec((1, width, hidden_dim), lambda i: (0, 0, 0)),
            pl.BlockSpec((1, width, hidden_dim), lambda i: (0, 0, 0)),
            pl.BlockSpec((1, hidden_dim, width), lambda i: (0, 0, 0)),
        ],
        out_specs=pl.BlockSpec((rows * PIECES, part), lambda i: (i, 0)),
        out_shape=jax.ShapeDtypeStruct((packed_rows, part), jnp.bfloat16),
        scratch_shapes=[
            pltpu.VMEM((PIECES, turn, turn * PIECES), jnp.bfloat16),
            pltpu.VMEM((PIECES, turn * PIECES, turn), jnp.bfloat16),
            pltpu.VMEM((rows, width), jnp.bfloat16),
            pltpu.VMEM((1, 128), jnp.float32),
        ],
        name="run_expert",
    )(keep_limit, arrived, gate_mat, up_mat, down_mat)


def swap(rows, devices):
    parts = rows.reshape(devices, -1, rows.shape[-1])
    return lax.all_to_all(parts, AXES, split_axis=0, concat_axis=0, tiled=True)


def body(tokens, expert_ids, gate_probs, capacity, flows, w_gate, w_up, w_down):
    devices = lax.axis_size(AXES)
    micros, tok, width = tokens.shape
    top = expert_ids.shape[2]
    ids = jnp.swapaxes(expert_ids, 1, 2)
    probs = jnp.swapaxes(gate_probs, 1, 2)
    slots = tok * top * 5 // (4 * devices)
    block_devices = 32
    keep_limit = capacity + jnp.sum(flows, 1)

    arrived = []
    for m in range(micros):
        packed = pack_tokens(tokens, ids, m)
        arrived.append(swap(packed, devices))
    answers = []
    for m in range(micros):
        incoming = arrived[m].reshape(-1, width // PIECES)
        returned = run_expert(incoming, keep_limit, w_gate, w_up, w_down, slots, block_devices)
        answers.append(swap(returned, devices))
    answered = [a.reshape(devices, PIECES + 1, TILE, width // PIECES) for a in answers]
    return mix_answers(answered, ids, probs)


def solution(mesh):
    placed = (
        P(None, AXES, None),
        P(None, AXES, None),
        P(None, AXES, None),
        P(AXES),
        P(AXES, None),
        P(AXES, None, None),
        P(AXES, None, None),
        P(AXES, None, None),
    )
    return jax.shard_map(
        body,
        mesh=mesh,
        in_specs=placed,
        out_specs=P(None, AXES, None),
        check_vma=False,
    )
```

```python
import jax
import jax.numpy as jnp
from jax import lax
from jax.experimental import pallas as pl
from jax.experimental.pallas import tpu as pltpu
from jax.sharding import PartitionSpec as P

AXES = ("expert", "group")
PIECES = 4
TILE = 8
MARK = 8.0


def iota(shape, dim):
    return lax.broadcasted_iota(jnp.int32, shape, dim)


def bit(condition):
    return jnp.where(condition, 1.0, 0.0)


def narrow(x):
    return x.astype(jnp.bfloat16)


def mm(a, b):
    return jnp.dot(a, b, preferred_element_type=jnp.float32)


def chosen_rank(ids, experts):
    top, tok = ids.shape
    expert = iota((experts, tok), 0)
    chosen = jnp.zeros((experts, tok), jnp.float32)
    for k in range(top):
        chosen = jnp.where(ids[k : k + 1, :] == expert, 1.0, chosen)
    before = mm(narrow(chosen), narrow(bit(iota((tok, tok), 0) < iota((tok, tok), 1))))
    return chosen * (before + 1.0)


def pack_tokens(tokens, ids, micro):
    _, tok, width = tokens.shape
    top = ids.shape[1]
    experts = lax.axis_size(AXES)
    part = width // PIECES
    rows = experts * TILE

    def kernel(ids_ref, tok_ref, out_ref, sent_ref, my_ids_ref, my_tok_ref, sems):
        def leave(q):
            return pltpu.make_async_copy(sent_ref.at[q], out_ref.at[:, q], sems.at[q])

        get_ids = pltpu.make_async_copy(ids_ref.at[micro], my_ids_ref, sems.at[PIECES + 1])
        get_ids.start()

        get_tokens = pltpu.make_async_copy(tok_ref.at[micro], my_tok_ref, sems.at[PIECES + 2])
        get_tokens.start()
        get_ids.wait()
        order = narrow(chosen_rank(my_ids_ref[...], experts))
        row = iota((rows, experts), 0)
        col = iota((rows, experts), 1)
        rank = mm(narrow(bit((row >> 3) == col)), order)
        inside = row & 7
        hit = bit(rank == (inside + 1).astype(jnp.float32))
        select = narrow(hit)
        first = col == 0
        mark = jnp.where((jnp.sum(hit, axis=1, keepdims=True) < 0.5) & first, MARK, 0.0)
        get_tokens.wait()
        for q in range(PIECES):
            moved = mm(select, my_tok_ref[:, q * part : (q + 1) * part])
            if q == 0:
                moved = jnp.concatenate([moved[:, :experts] + mark, moved[:, experts:]], axis=1)
            sent_ref[q] = narrow(moved.reshape(experts, TILE, part))
            leave(q).start()
        hit = bit(rank == ((inside >> 2) + (TILE + 1)).astype(jnp.float32))
        piece = inside & 3
        select = jnp.concatenate([narrow(jnp.where(piece == q, hit, 0.0)) for q in range(PIECES)], axis=1)
        stacked = jnp.concatenate([my_tok_ref[:, q * part : (q + 1) * part] for q in range(PIECES)], axis=0)
        moved = mm(select, stacked)
        mark = jnp.where((jnp.sum(hit, axis=1, keepdims=True) < 0.5) & first & (piece == 0), MARK, 0.0)
        moved = jnp.concatenate([moved[:, :experts] + mark, moved[:, experts:]], axis=1)
        sent_ref[PIECES] = narrow(moved.reshape(experts, TILE, part))
        leave(PIECES).start()
        for q in range(PIECES + 1):
            leave(q).wait()

    return pl.pallas_call(
        kernel,
        grid=(1,),
        in_specs=[pl.BlockSpec(memory_space=pl.ANY)] * 2,
        out_specs=pl.BlockSpec(memory_space=pl.ANY),
        out_shape=jax.ShapeDtypeStruct((experts, PIECES + 1, TILE, part), jnp.bfloat16),
        scratch_shapes=[
            pltpu.VMEM((PIECES + 1, experts, TILE, part), jnp.bfloat16),
            pltpu.VMEM((top, tok), ids.dtype),
            pltpu.VMEM((tok, width), jnp.bfloat16),
            pltpu.SemaphoreType.DMA((PIECES + 3,)),
        ],
        name="pack_tokens",
    )(ids, tokens)


def mix_answers(answered, ids, probs, micro, earlier_out):
    micros, top, tok = ids.shape
    experts = lax.axis_size(AXES)
    part = answered.shape[3]
    width = part * PIECES
    rows = experts * TILE

    def kernel(ids_ref, probs_ref, rows_ref, *rest):
        out_ref, here_ref, my_ids_ref, my_probs_ref, sum_ref, sems = rest[-6:]

        def leave(q):
            columns = out_ref.at[micro, :, pl.ds(q * part, part)]
            return pltpu.make_async_copy(sum_ref.at[q], columns, sems.at[PIECES + 3 + q])

        def fetch(q):
            return pltpu.make_async_copy(rows_ref.at[:, q], here_ref.at[q], sems.at[q])

        get_ids = pltpu.make_async_copy(ids_ref.at[micro], my_ids_ref, sems.at[PIECES + 1])
        get_probs = pltpu.make_async_copy(probs_ref.at[micro], my_probs_ref, sems.at[PIECES + 2])
        get_ids.start()
        get_probs.start()
        for q in (PIECES, *range(PIECES)):
            fetch(q).start()
        get_ids.wait()
        get_probs.wait()
        ids_here = my_ids_ref[...]
        probs_here = my_probs_ref[...]
        norm = probs_here / jnp.sum(probs_here, axis=0, keepdims=True)
        expert = iota((experts, tok), 0)
        gate = jnp.zeros((experts, tok), jnp.float32)
        for k in range(top):
            gate = jnp.where(ids_here[k : k + 1, :] == expert, norm[k : k + 1, :], gate)
        spread = narrow(bit((iota((experts, rows), 1) >> 3) == iota((experts, rows), 0)))
        rank = mm(narrow(chosen_rank(ids_here, experts).T), spread)
        gate = mm(narrow(gate.T), spread)
        inside = iota((tok, rows), 1) & 7
        weight = narrow(jnp.where(rank == (inside + 1).astype(jnp.float32), gate, 0.0))
        rest_weight = jnp.where(rank == ((inside >> 2) + (TILE + 1)).astype(jnp.float32), gate, 0.0)
        rest_weight = jnp.concatenate(
            [narrow(jnp.where((inside & 3) == q, rest_weight, 0.0)) for q in range(PIECES)], axis=0
        )
        fetch(PIECES).wait()
        last = mm(rest_weight, here_ref[PIECES].reshape(rows, part))
        for q in range(PIECES):
            fetch(q).wait()
            main = mm(weight, here_ref[q].reshape(rows, part))
            sum_ref[q] = narrow(main + last[q * tok : (q + 1) * tok])
            leave(q).start()
        for q in range(PIECES):
            leave(q).wait()

    in_specs = [pl.BlockSpec(memory_space=pl.ANY)] * 3
    operands = [ids, probs, answered]
    aliases = {}
    if earlier_out is not None:
        in_specs.append(pl.BlockSpec(memory_space=pl.ANY))
        operands.append(earlier_out)
        aliases = {3: 0}
    return pl.pallas_call(
        kernel,
        grid=(1,),
        in_specs=in_specs,
        out_specs=pl.BlockSpec(memory_space=pl.ANY),
        out_shape=jax.ShapeDtypeStruct((micros, tok, width), jnp.bfloat16),
        scratch_shapes=[
            pltpu.VMEM((PIECES + 1, experts, TILE, part), jnp.bfloat16),
            pltpu.VMEM((top, tok), ids.dtype),
            pltpu.VMEM((top, tok), probs.dtype),
            pltpu.VMEM((PIECES, tok, part), jnp.bfloat16),
            pltpu.SemaphoreType.DMA((2 * PIECES + 3,)),
        ],
        input_output_aliases=aliases,
        name="mix_answers",
    )(*operands)


def place(row, slots, q):
    device = jnp.floor((row.astype(jnp.float32) + 0.5) * (1.0 / slots)).astype(jnp.int32)
    slot = row - device * slots
    inside = jnp.where(slot < TILE, q * TILE + slot, slot * PIECES + q)
    return device * slots * PIECES + inside


def run_expert(arrived, keep_limit, gate_mat, up_mat, down_mat, slots, block_devices):
    packed_rows, part = arrived.shape
    width, hidden_dim = gate_mat.shape[1:]
    turn = 16 * slots
    turns = block_devices * slots // turn
    rows = block_devices * slots
    steps = packed_rows // (rows * PIECES)

    def kernel(limit_ref, in_ref, gate_ref, up_ref, down_ref, out_ref, join_ref, split_ref, rows_ref, seen_ref):
        step = pl.program_id(0)

        @pl.when(step == 0)
        def _():
            seen_ref[...] = jnp.zeros_like(seen_ref)
            for q in range(PIECES):
                shape = (turn, turn * PIECES)
                join_ref[q] = narrow(bit(place(iota(shape, 0), slots, q) == iota(shape, 1)))
                shape = (turn * PIECES, turn)
                split_ref[q] = narrow(bit(place(iota(shape, 1), slots, q) == iota(shape, 0)))

        for j in range(turns):
            pieces = in_ref[j * turn * PIECES : (j + 1) * turn * PIECES, :]
            for q in range(PIECES):
                rows_ref[j * turn : (j + 1) * turn, q * part : (q + 1) * part] = jnp.dot(
                    join_ref[q], pieces, preferred_element_type=jnp.float32
                ).astype(jnp.bfloat16)
        rows_here = rows_ref[...]
        lanes = seen_ref.shape[1]
        live = jnp.where(
            jnp.broadcast_to(rows_here[:, :1].astype(jnp.float32), (rows, lanes)) < MARK - 1.0, 1.0, 0.0
        )
        above = lax.broadcasted_iota(jnp.int32, (rows, rows), 0) > lax.broadcasted_iota(jnp.int32, (rows, rows), 1)
        rank = seen_ref[...] + jnp.dot(
            jnp.where(above, 1.0, 0.0).astype(jnp.bfloat16),
            live.astype(jnp.bfloat16),
            preferred_element_type=jnp.float32,
        )
        seen_ref[...] += jnp.sum(live, axis=0, keepdims=True)
        limit = limit_ref[0].astype(jnp.float32)
        kept = (live > 0.5) & (rank < limit)
        kept = jnp.where(kept, 1.0, 0.0)[:, :1] > 0.5

        gate_val = jnp.dot(rows_here, gate_ref[0], preferred_element_type=jnp.float32)
        up_val = jnp.dot(rows_here, up_ref[0], preferred_element_type=jnp.float32)
        hidden = (gate_val * lax.logistic(gate_val) * up_val).astype(jnp.bfloat16)
        out_val = jnp.dot(hidden, down_ref[0], preferred_element_type=jnp.float32)
        out_val = jnp.where(kept, out_val, 0.0).astype(jnp.bfloat16)
        for j in range(turns):
            moved = jnp.zeros((turn * PIECES, part), jnp.float32)
            for q in range(PIECES):
                moved = moved + jnp.dot(
                    split_ref[q],
                    out_val[j * turn : (j + 1) * turn, q * part : (q + 1) * part],
                    preferred_element_type=jnp.float32,
                )
            out_ref[j * turn * PIECES : (j + 1) * turn * PIECES, :] = moved.astype(jnp.bfloat16)

    return pl.pallas_call(
        kernel,
        grid=(steps,),
        in_specs=[
            pl.BlockSpec(memory_space=pltpu.SMEM),
            pl.BlockSpec((rows * PIECES, part), lambda i: (i, 0)),
            pl.BlockSpec((1, width, hidden_dim), lambda i: (0, 0, 0)),
            pl.BlockSpec((1, width, hidden_dim), lambda i: (0, 0, 0)),
            pl.BlockSpec((1, hidden_dim, width), lambda i: (0, 0, 0)),
        ],
        out_specs=pl.BlockSpec((rows * PIECES, part), lambda i: (i, 0)),
        out_shape=jax.ShapeDtypeStruct((packed_rows, part), jnp.bfloat16),
        scratch_shapes=[
            pltpu.VMEM((PIECES, turn, turn * PIECES), jnp.bfloat16),
            pltpu.VMEM((PIECES, turn * PIECES, turn), jnp.bfloat16),
            pltpu.VMEM((rows, width), jnp.bfloat16),
            pltpu.VMEM((1, 128), jnp.float32),
        ],
        name="run_expert",
    )(keep_limit, arrived, gate_mat, up_mat, down_mat)


def swap(rows, devices):
    parts = rows.reshape(devices, -1, rows.shape[-1])
    return lax.all_to_all(parts, AXES, split_axis=0, concat_axis=0, tiled=True)


def body(tokens, expert_ids, gate_probs, capacity, flows, w_gate, w_up, w_down):
    devices = lax.axis_size(AXES)
    micros, tok, width = tokens.shape
    top = expert_ids.shape[2]
    ids = jnp.swapaxes(expert_ids, 1, 2)
    probs = jnp.swapaxes(gate_probs, 1, 2)
    slots = tok * top * 5 // (4 * devices)
    block_devices = 32
    keep_limit = capacity + jnp.sum(flows, 1)

    arrived = []
    for m in range(micros):
        packed = pack_tokens(tokens, ids, m)
        arrived.append(swap(packed, devices))
    answers = []
    for m in range(micros):
        incoming = arrived[m].reshape(-1, width // PIECES)
        returned = run_expert(incoming, keep_limit, w_gate, w_up, w_down, slots, block_devices)
        answers.append(swap(returned, devices))
    out = None
    for m in range(micros):
        answered = answers[m].reshape(devices, PIECES + 1, TILE, width // PIECES)
        out = mix_answers(answered, ids, probs, m, out)
    return out


def solution(mesh):
    placed = (
        P(None, AXES, None),
        P(None, AXES, None),
        P(None, AXES, None),
        P(AXES),
        P(AXES, None),
        P(AXES, None, None),
        P(AXES, None, None),
        P(AXES, None, None),
    )
    return jax.shard_map(
        body,
        mesh=mesh,
        in_specs=placed,
        out_specs=P(None, AXES, None),
        check_vma=False,
    )
```

```python
import jax
import jax.numpy as jnp
from jax import lax
from jax.experimental import pallas as pl
from jax.experimental.pallas import tpu as pltpu
from jax.sharding import PartitionSpec as P

AXES = ("expert", "group")
PIECES = 4
TILE = 8
MARK = 8.0


def iota(shape, dim):
    return lax.broadcasted_iota(jnp.int32, shape, dim)


def bit(condition):
    return jnp.where(condition, 1.0, 0.0)


def narrow(x):
    return x.astype(jnp.bfloat16)


def mm(a, b):
    return jnp.dot(a, b, preferred_element_type=jnp.float32)


def chosen_rank(ids, experts):
    top, tok = ids.shape
    expert = iota((experts, tok), 0)
    chosen = jnp.zeros((experts, tok), jnp.float32)
    for k in range(top):
        chosen = jnp.where(ids[k : k + 1, :] == expert, 1.0, chosen)
    before = mm(narrow(chosen), narrow(bit(iota((tok, tok), 0) < iota((tok, tok), 1))))
    return chosen * (before + 1.0)


def pack_tokens(tokens, ids, micro):
    _, tok, width = tokens.shape
    top = ids.shape[1]
    experts = lax.axis_size(AXES)
    part = width // PIECES
    rows = experts * TILE

    def kernel(ids_ref, tok_ref, out_ref, sent_ref, my_ids_ref, my_tok_ref, sems):
        def leave(q):
            return pltpu.make_async_copy(sent_ref.at[q], out_ref.at[:, q], sems.at[q])

        get_ids = pltpu.make_async_copy(ids_ref.at[micro], my_ids_ref, sems.at[PIECES + 1])
        get_ids.start()

        get_tokens = pltpu.make_async_copy(tok_ref.at[micro], my_tok_ref, sems.at[PIECES + 2])
        get_tokens.start()
        get_ids.wait()
        order = narrow(chosen_rank(my_ids_ref[...], experts))
        row = iota((rows, experts), 0)
        col = iota((rows, experts), 1)
        rank = mm(narrow(bit((row >> 3) == col)), order)
        inside = row & 7
        hit = bit(rank == (inside + 1).astype(jnp.float32))
        select = narrow(hit)
        first = col == 0
        get_tokens.wait()
        for q in (*range(1, PIECES), 0):
            moved = mm(select, my_tok_ref[:, q * part : (q + 1) * part])
            if q == 0:
                mark = jnp.where((jnp.sum(hit, axis=1, keepdims=True) < 0.5) & first, MARK, 0.0)
                moved = jnp.concatenate([moved[:, :experts] + mark, moved[:, experts:]], axis=1)
            sent_ref[q] = narrow(moved.reshape(experts, TILE, part))
            leave(q).start()
        hit = bit(rank == ((inside >> 2) + (TILE + 1)).astype(jnp.float32))
        piece = inside & 3
        select = jnp.concatenate([narrow(jnp.where(piece == q, hit, 0.0)) for q in range(PIECES)], axis=1)
        stacked = jnp.concatenate([my_tok_ref[:, q * part : (q + 1) * part] for q in range(PIECES)], axis=0)
        moved = mm(select, stacked)
        mark = jnp.where((jnp.sum(hit, axis=1, keepdims=True) < 0.5) & first & (piece == 0), MARK, 0.0)
        moved = jnp.concatenate([moved[:, :experts] + mark, moved[:, experts:]], axis=1)
        sent_ref[PIECES] = narrow(moved.reshape(experts, TILE, part))
        leave(PIECES).start()
        for q in range(PIECES + 1):
            leave(q).wait()

    return pl.pallas_call(
        kernel,
        grid=(1,),
        in_specs=[pl.BlockSpec(memory_space=pl.ANY)] * 2,
        out_specs=pl.BlockSpec(memory_space=pl.ANY),
        out_shape=jax.ShapeDtypeStruct((experts, PIECES + 1, TILE, part), jnp.bfloat16),
        scratch_shapes=[
            pltpu.VMEM((PIECES + 1, experts, TILE, part), jnp.bfloat16),
            pltpu.VMEM((top, tok), ids.dtype),
            pltpu.VMEM((tok, width), jnp.bfloat16),
            pltpu.SemaphoreType.DMA((PIECES + 3,)),
        ],
        name="pack_tokens",
    )(ids, tokens)


def mix_answers(answered, ids, probs, micro, earlier_out):
    micros, top, tok = ids.shape
    experts = lax.axis_size(AXES)
    part = answered.shape[3]
    width = part * PIECES
    rows = experts * TILE

    def kernel(ids_ref, probs_ref, rows_ref, *rest):
        out_ref, here_ref, my_ids_ref, my_probs_ref, sum_ref, sems = rest[-6:]

        def leave(q):
            columns = out_ref.at[micro, :, pl.ds(q * part, part)]
            return pltpu.make_async_copy(sum_ref.at[q], columns, sems.at[PIECES + 3 + q])

        def fetch(q):
            return pltpu.make_async_copy(rows_ref.at[:, q], here_ref.at[q], sems.at[q])

        get_ids = pltpu.make_async_copy(ids_ref.at[micro], my_ids_ref, sems.at[PIECES + 1])
        get_probs = pltpu.make_async_copy(probs_ref.at[micro], my_probs_ref, sems.at[PIECES + 2])
        get_ids.start()
        get_probs.start()
        for q in (PIECES, *range(PIECES)):
            fetch(q).start()
        get_ids.wait()
        get_probs.wait()
        ids_here = my_ids_ref[...]
        probs_here = my_probs_ref[...]
        norm = probs_here / jnp.sum(probs_here, axis=0, keepdims=True)
        expert = iota((experts, tok), 0)
        gate = jnp.zeros((experts, tok), jnp.float32)
        for k in range(top):
            gate = jnp.where(ids_here[k : k + 1, :] == expert, norm[k : k + 1, :], gate)
        spread = narrow(bit((iota((experts, rows), 1) >> 3) == iota((experts, rows), 0)))
        rank = mm(narrow(chosen_rank(ids_here, experts).T), spread)
        gate = mm(narrow(gate.T), spread)
        inside = iota((tok, rows), 1) & 7
        weight = narrow(jnp.where(rank == (inside + 1).astype(jnp.float32), gate, 0.0))
        rest_weight = jnp.where(rank == ((inside >> 2) + (TILE + 1)).astype(jnp.float32), gate, 0.0)
        rest_weight = jnp.concatenate(
            [narrow(jnp.where((inside & 3) == q, rest_weight, 0.0)) for q in range(PIECES)], axis=0
        )
        fetch(PIECES).wait()
        last = mm(rest_weight, here_ref[PIECES].reshape(rows, part))
        for q in range(PIECES):
            fetch(q).wait()
            main = mm(weight, here_ref[q].reshape(rows, part))
            sum_ref[q] = narrow(main + last[q * tok : (q + 1) * tok])
            leave(q).start()
        for q in range(PIECES):
            leave(q).wait()

    in_specs = [pl.BlockSpec(memory_space=pl.ANY)] * 3
    operands = [ids, probs, answered]
    aliases = {}
    if earlier_out is not None:
        in_specs.append(pl.BlockSpec(memory_space=pl.ANY))
        operands.append(earlier_out)
        aliases = {3: 0}
    return pl.pallas_call(
        kernel,
        grid=(1,),
        in_specs=in_specs,
        out_specs=pl.BlockSpec(memory_space=pl.ANY),
        out_shape=jax.ShapeDtypeStruct((micros, tok, width), jnp.bfloat16),
        scratch_shapes=[
            pltpu.VMEM((PIECES + 1, experts, TILE, part), jnp.bfloat16),
            pltpu.VMEM((top, tok), ids.dtype),
            pltpu.VMEM((top, tok), probs.dtype),
            pltpu.VMEM((PIECES, tok, part), jnp.bfloat16),
            pltpu.SemaphoreType.DMA((2 * PIECES + 3,)),
        ],
        input_output_aliases=aliases,
        name="mix_answers",
    )(*operands)


def place(row, slots, q):
    device = jnp.floor((row.astype(jnp.float32) + 0.5) * (1.0 / slots)).astype(jnp.int32)
    slot = row - device * slots
    inside = jnp.where(slot < TILE, q * TILE + slot, slot * PIECES + q)
    return device * slots * PIECES + inside


def run_expert(arrived, keep_limit, gate_mat, up_mat, down_mat, slots, block_devices):
    packed_rows, part = arrived.shape
    width, hidden_dim = gate_mat.shape[1:]
    turn = 16 * slots
    turns = block_devices * slots // turn
    rows = block_devices * slots
    steps = packed_rows // (rows * PIECES)

    def kernel(limit_ref, in_ref, gate_ref, up_ref, down_ref, out_ref, join_ref, split_ref, rows_ref, seen_ref):
        step = pl.program_id(0)

        @pl.when(step == 0)
        def _():
            seen_ref[...] = jnp.zeros_like(seen_ref)
            for q in range(PIECES):
                shape = (turn, turn * PIECES)
                join_ref[q] = narrow(bit(place(iota(shape, 0), slots, q) == iota(shape, 1)))
                shape = (turn * PIECES, turn)
                split_ref[q] = narrow(bit(place(iota(shape, 1), slots, q) == iota(shape, 0)))

        for j in range(turns):
            pieces = in_ref[j * turn * PIECES : (j + 1) * turn * PIECES, :]
            for q in range(PIECES):
                rows_ref[j * turn : (j + 1) * turn, q * part : (q + 1) * part] = jnp.dot(
                    join_ref[q], pieces, preferred_element_type=jnp.float32
                ).astype(jnp.bfloat16)
        rows_here = rows_ref[...]
        lanes = seen_ref.shape[1]
        live = jnp.where(
            jnp.broadcast_to(rows_here[:, :1].astype(jnp.float32), (rows, lanes)) < MARK - 1.0, 1.0, 0.0
        )
        above = lax.broadcasted_iota(jnp.int32, (rows, rows), 0) > lax.broadcasted_iota(jnp.int32, (rows, rows), 1)
        rank = seen_ref[...] + jnp.dot(
            jnp.where(above, 1.0, 0.0).astype(jnp.bfloat16),
            live.astype(jnp.bfloat16),
            preferred_element_type=jnp.float32,
        )
        seen_ref[...] += jnp.sum(live, axis=0, keepdims=True)
        limit = limit_ref[0].astype(jnp.float32)
        kept = (live > 0.5) & (rank < limit)
        kept = jnp.where(kept, 1.0, 0.0)[:, :1] > 0.5

        gate_val = jnp.dot(rows_here, gate_ref[0], preferred_element_type=jnp.float32)
        up_val = jnp.dot(rows_here, up_ref[0], preferred_element_type=jnp.float32)
        hidden = (gate_val * lax.logistic(gate_val) * up_val).astype(jnp.bfloat16)
        out_val = jnp.dot(hidden, down_ref[0], preferred_element_type=jnp.float32)
        out_val = jnp.where(kept, out_val, 0.0).astype(jnp.bfloat16)
        for j in range(turns):
            moved = jnp.zeros((turn * PIECES, part), jnp.float32)
            for q in range(PIECES):
                moved = moved + jnp.dot(
                    split_ref[q],
                    out_val[j * turn : (j + 1) * turn, q * part : (q + 1) * part],
                    preferred_element_type=jnp.float32,
                )
            out_ref[j * turn * PIECES : (j + 1) * turn * PIECES, :] = moved.astype(jnp.bfloat16)

    return pl.pallas_call(
        kernel,
        grid=(steps,),
        in_specs=[
            pl.BlockSpec(memory_space=pltpu.SMEM),
            pl.BlockSpec((rows * PIECES, part), lambda i: (i, 0)),
            pl.BlockSpec((1, width, hidden_dim), lambda i: (0, 0, 0)),
            pl.BlockSpec((1, width, hidden_dim), lambda i: (0, 0, 0)),
            pl.BlockSpec((1, hidden_dim, width), lambda i: (0, 0, 0)),
        ],
        out_specs=pl.BlockSpec((rows * PIECES, part), lambda i: (i, 0)),
        out_shape=jax.ShapeDtypeStruct((packed_rows, part), jnp.bfloat16),
        scratch_shapes=[
            pltpu.VMEM((PIECES, turn, turn * PIECES), jnp.bfloat16),
            pltpu.VMEM((PIECES, turn * PIECES, turn), jnp.bfloat16),
            pltpu.VMEM((rows, width), jnp.bfloat16),
            pltpu.VMEM((1, 128), jnp.float32),
        ],
        name="run_expert",
    )(keep_limit, arrived, gate_mat, up_mat, down_mat)


def swap(rows, devices):
    parts = rows.reshape(devices, -1, rows.shape[-1])
    return lax.all_to_all(parts, AXES, split_axis=0, concat_axis=0, tiled=True)


def body(tokens, expert_ids, gate_probs, capacity, flows, w_gate, w_up, w_down):
    devices = lax.axis_size(AXES)
    micros, tok, width = tokens.shape
    top = expert_ids.shape[2]
    ids = jnp.swapaxes(expert_ids, 1, 2)
    probs = jnp.swapaxes(gate_probs, 1, 2)
    slots = tok * top * 5 // (4 * devices)
    block_devices = 32
    keep_limit = capacity + jnp.sum(flows, 1)

    arrived = []
    for m in range(micros):
        packed = pack_tokens(tokens, ids, m)
        arrived.append(swap(packed, devices))
    answers = []
    for m in range(micros):
        incoming = arrived[m].reshape(-1, width // PIECES)
        returned = run_expert(incoming, keep_limit, w_gate, w_up, w_down, slots, block_devices)
        answers.append(swap(returned, devices))
    out = None
    for m in range(micros):
        answered = answers[m].reshape(devices, PIECES + 1, TILE, width // PIECES)
        out = mix_answers(answered, ids, probs, m, out)
    return out


def solution(mesh):
    placed = (
        P(None, AXES, None),
        P(None, AXES, None),
        P(None, AXES, None),
        P(AXES),
        P(AXES, None),
        P(AXES, None, None),
        P(AXES, None, None),
        P(AXES, None, None),
    )
    return jax.shard_map(
        body,
        mesh=mesh,
        in_specs=placed,
        out_specs=P(None, AXES, None),
        check_vma=False,
    )
```
